32 devices in a mesh: shot: 2 (over x), freq: 8 (over z, y), tile: 2 (over core).
Axes of the slice: x: 2, y: 2, z: 4, core: 2. Of those that a mesh axis runs over, the one named last changes fastest.
Arguments:
- source_field: float32 [4, 8, 64, 1024], P('shot', 'freq', 'tile'), parts along dimension 0, may hold values from -6 to 6
- receiver_field: float32 [4, 8, 64, 1024], P('shot', 'freq', 'tile'), parts along dimension 0, may hold values from -6 to 6
- slowness: float32 [3, 64, 1024], P(None, 'tile', 'freq'), may hold values from 0.5 to 2
- omegas: float32 [8], P('freq'), may hold values from 1.5 to 5
Outputs:
- image_steps: float32 [6, 64, 1024], P('shot', 'tile'), parts along dimension 0
- illumination: float32 [6, 64, 1024], P('shot', 'tile'), parts along dimension 0
The draws below stay inside these ranges and needn't reach their ends.
There are 2 independent parts, one for each index of `shot`. The reference program is written for one: setup_inputs(seed, part) draws one part's arguments, and reference() takes and returns one part's arrays. A program takes and returns all parts, laid end to end along the dimension named above; an argument that names none is the same for every part. Nothing has to cross between parts.
All inputs are finite; a program needn't handle non-finite values.
Results may differ from the reference program's by a relative error of at most 0.0003.
Values sent between devices are 32-bit elements; how exact they have to be, the bound alone decides.
A program may use at most 64 MiB of HBM per device.

```python
import math
import jax
import jax.numpy as jnp
from jax import lax

NY = 1024
STEPS = 3
TERMS = 10
NODES = 16
NF = 8
NX = 64


def block_levels(rng, dims, shards, least, high):
    gain = 1.0
    for axis_at, shards_of in shards:
        steps = jax.random.uniform(jax.random.fold_in(jax.random.fold_in(rng, 6), axis_at), (shards_of,), jnp.float32, least / len(shards), high / len(shards))
        gain = gain * jnp.repeat(jnp.exp(steps), dims[axis_at] // shards_of).reshape((-1,) + (1,) * (len(dims) - 1 - axis_at))
    return gain


def centred(key, extent, width, most, split=(), held_as=jnp.bfloat16):
    level = block_levels(key, extent, split, -0.22, 0.18) if split else 1.0
    array = jax.random.normal(key, extent, jnp.float32) * width * level
    return jnp.minimum(jnp.maximum(array, -most), most).astype(held_as)


def setup_inputs(seed: int = 0, part: int = 0) -> dict:
    keys = jax.random.split(jax.random.key(seed), 5)
    own_keys = jax.random.split(jax.random.fold_in(keys[4], part), 5)
    return {
        "source_field": centred(own_keys[0], (2, NF, NX, NY), 1.0, 6.0, ((1, 8), (2, 2)), jnp.float32),
        "receiver_field": centred(own_keys[1], (2, NF, NX, NY), 1.0, 6.0, ((1, 8), (2, 2)), jnp.float32),
        "slowness": jnp.clip(0.5 + 1.5 * jax.random.uniform(keys[2], (STEPS, NX, NY), jnp.float32) ** block_levels(keys[2], (STEPS, NX, NY), ((1, 2), (2, 8)), -0.2, 0.2), 0.5, 2.0),
        "omegas": jnp.clip(jnp.exp(math.log(5.0) - 1.2039728 * jax.random.uniform(keys[3], (NF,), jnp.float32) ** block_levels(keys[3], (NF,), ((0, 8),), -0.2, 0.2)), 1.5, 5.0),
    }


def mcclellan_rows(padded):
    along_x = 0.5 * padded[:, :, :-2] + padded[:, :, 1:-1] + 0.5 * padded[:, :, 2:]
    widened = jnp.pad(along_x, ((0, 0), (0, 0), (0, 0), (1, 1)))
    along_y = 0.5 * widened[..., :-2] + widened[..., 1:-1] + 0.5 * widened[..., 2:]
    return 0.5 * along_y - padded[:, :, 1:-1]

def mcclellan_full(fields):
    return mcclellan_rows(jnp.pad(fields, ((0, 0), (0, 0), (1, 1), (0, 0))))

def coefficients(omega_values, slow_slab):
    node_angles = (jnp.arange(NODES, dtype=jnp.float32) + 0.5) * (math.pi / NODES)
    orders = jnp.arange(TERMS, dtype=jnp.float32)
    weights = jnp.where(orders == 0, 1.0, 2.0) / NODES
    cheb_table = jnp.cos(node_angles[:, None] * orders[None, :]) * weights[None, :]
    phase_arg = omega_values[:, None, None, None] * jnp.cos(node_angles)[None, :, None, None] * slow_slab[None, None]
    coef_real = jnp.einsum('fmxy,mn->fnxy', jnp.cos(phase_arg), cheb_table, precision=lax.Precision.HIGHEST)
    coef_imag = jnp.einsum('fmxy,mn->fnxy', jnp.sin(phase_arg), cheb_table, precision=lax.Precision.HIGHEST)
    return (coef_real, coef_imag)

def apply_terms(summed, coef_real, coef_imag, cheb_term):
    source_real, source_imag, receiver_real, receiver_imag = (cheb_term[0], cheb_term[1], cheb_term[2], cheb_term[3])
    return summed + jnp.stack([coef_real * source_real - coef_imag * source_imag, coef_real * source_imag + coef_imag * source_real, coef_real * receiver_real + coef_imag * receiver_imag, coef_real * receiver_imag - coef_imag * receiver_real])

def extrapolate(fields, coef_real, coef_imag):
    prev_term = fields
    this_term = mcclellan_full(fields)
    summed = apply_terms(jnp.zeros_like(fields), coef_real[:, 0], coef_imag[:, 0], prev_term)
    summed = apply_terms(summed, coef_real[:, 1], coef_imag[:, 1], this_term)
    for term_order in range(2, TERMS):
        next_term = 2.0 * mcclellan_full(this_term) - prev_term
        summed = apply_terms(summed, coef_real[:, term_order], coef_imag[:, term_order], next_term)
        prev_term, this_term = (this_term, next_term)
    return summed

def reference(source_field, receiver_field, slowness, omegas):
    fields = jnp.concatenate([source_field, receiver_field], 0)
    image_list = []
    energy_list = []
    for depth_index in range(STEPS):
        coef_real, coef_imag = coefficients(omegas, slowness[depth_index])
        fields = extrapolate(fields, coef_real, coef_imag)
        image_list.append(lax.optimization_barrier(jnp.sum(fields[0] * fields[2] + fields[1] * fields[3], axis=0)) / math.sqrt(NF))
        energy_list.append(lax.optimization_barrier(jnp.sum(fields[0] * fields[0] + fields[1] * fields[1], axis=0)) / NF)
    return (jnp.stack(image_list), jnp.stack(energy_list))
```

```python
import functools
import math

import jax
import jax.numpy as jnp
import numpy as np
from jax import lax
from jax.experimental import pallas as pl
from jax.experimental.pallas import tpu as pltpu
from jax.sharding import PartitionSpec as P

TERMS = 10
NODES = 16
MARGIN = TERMS - 1
HALF = NODES // 2
SUB, LANE = 8, 128
MESH = pl.DeviceIdType.MESH
UNROLL = 4

SIN_POLY = (3.14159258, -5.16770688, 2.55003137, -0.59804516, 0.07722009)
COS_POLY = (0.99999995, -4.93479286, 4.0584119, -1.33188005, 0.21969657)


def horner(coefs, z):
    out = coefs[-1] * z + coefs[-2]
    for c in reversed(coefs[:-2]):
        out = out * z + c
    return out


def folded_coefficients(u):
    theta = [math.pi * (m + 0.5) / NODES for m in range(HALF)]
    cosines, sines = [], []
    for m in range(HALF):
        y = u * (math.cos(theta[m]) / (2 * math.pi))
        g = y - jnp.round(y)
        z = g * g
        s = horner(SIN_POLY, z) * g
        c = horner(COS_POLY, z)
        twice = s + s
        cosines.append(1.0 - twice * s)
        sines.append(twice * c)
    weight = [2.0 * (1.0 if n == 0 else 2.0) / NODES for n in range(TERMS)]
    out = [None] * TERMS
    sums = [cosines[m] + cosines[HALF - 1 - m] for m in range(HALF // 2)]
    diffs = [cosines[m] - cosines[HALF - 1 - m] for m in range(HALF // 2)]
    for n in range(0, TERMS, 2):
        terms = sums if (n // 2) % 2 == 0 else diffs
        total = None
        for m in range(HALF // 2):
            term = terms[m] * (weight[n] * math.cos(n * theta[m]))
            total = term if total is None else total + term
        out[n] = total
    for n in range(1, TERMS, 2):
        total = None
        for m in range(HALF):
            term = sines[m] * (weight[n] * math.cos(n * theta[m]))
            total = term if total is None else total + term
        out[n] = total
    return out


def kernel(cfg, src_ref, rec_ref, slow_ref, omega_ref, out_ref, base, terms, gathered, part,
           recv1, acc1, recv2, result, load_sem, own_sem, out_sem, slow_send, slow_recv,
           halo_send, halo_recv, s1_send, s1_recv, s2_send, s2_recv,
           gz_send, gz_recv, gy_send, gy_recv):
    n, g1, g2, rows, steps, freq_total, cols = cfg
    half, chunk = rows // g1, rows // (g1 * g2)
    fi = lax.axis_index("freq")
    ti = lax.axis_index("tile")
    yi, zi = lax.rem(fi, g1), lax.div(fi, g1)
    other_y = g1 - 1 - yi

    def freq_at(y, z):
        return {"freq": z * g1 + y}

    loads = [
        pltpu.make_async_copy(src_ref, base.at[0, 0:2, pl.ds(MARGIN, rows)], load_sem.at[0]),
        pltpu.make_async_copy(rec_ref, base.at[0, 2:4, pl.ds(MARGIN, rows)], load_sem.at[1]),
        pltpu.make_async_copy(slow_ref, gathered.at[fi], own_sem),
    ]
    for copy in loads:
        copy.start()

    barrier = pltpu.get_barrier_semaphore()
    for j in range(1, n):
        pl.semaphore_signal(barrier, inc=1, device_id={"freq": lax.rem(fi + j, n)}, device_id_type=MESH)
    pl.semaphore_signal(barrier, inc=1, device_id={"tile": 1 - ti}, device_id_type=MESH)

    zero_row = jnp.where(ti == 0, MARGIN - 1, MARGIN + rows)
    zero = jnp.zeros((SUB, LANE), jnp.float32)
    for f in range(4):
        for d in range(steps):
            base[d, f, zero_row] = zero
        for t in range(TERMS - 1):
            terms[t, f, zero_row] = zero

    pl.semaphore_wait(barrier, n)

    in_start = jnp.where(ti == 0, rows - MARGIN, 0)
    halo_src = in_start + MARGIN
    halo_dst = jnp.where(ti == 0, 0, MARGIN + rows)

    def halo_copies(d):
        dst = pl.ds(halo_dst, MARGIN)
        if d == 0:
            pairs = [
                (src_ref.at[:, pl.ds(in_start, MARGIN)], base.at[0, 0:2, dst]),
                (rec_ref.at[:, pl.ds(in_start, MARGIN)], base.at[0, 2:4, dst]),
            ]
        else:
            pairs = [
                (base.at[d, 0:2, pl.ds(halo_src, MARGIN)], base.at[d, 0:2, dst]),
                (base.at[d, 2:4, pl.ds(halo_src, MARGIN)], base.at[d, 2:4, dst]),
            ]
        return [
            pltpu.make_async_remote_copy(
                src_ref=a, dst_ref=b, send_sem=halo_send.at[d, i], recv_sem=halo_recv.at[d, i],
                device_id={"tile": 1 - ti}, device_id_type=MESH)
            for i, (a, b) in enumerate(pairs)
        ]

    def slow_copy(d, slot, j, target):
        return pltpu.make_async_remote_copy(
            src_ref=slow_ref.at[d], dst_ref=gathered.at[slot, d],
            send_sem=slow_send.at[d, j], recv_sem=slow_recv.at[d, slot],
            device_id={"freq": target}, device_id_type=MESH)

    for copy in halo_copies(0):
        copy.start()
    for d in range(steps):
        for j in range(1, n):
            slow_copy(d, fi, j, lax.rem(fi + j, n)).start()

    for copy in loads[:2]:
        copy.wait()

    lane = lax.broadcasted_iota(jnp.int32, (SUB, LANE), 1)
    sub = lax.broadcasted_iota(jnp.int32, (SUB, LANE), 0)
    lane_lo, lane_hi = lane == 0, lane == LANE - 1
    edge_lo, edge_hi = sub == 0, sub == SUB - 1

    def neighbours(v):
        left = pltpu.roll(v, 1, 1)
        right = pltpu.roll(v, LANE - 1, 1)
        left_carry = jnp.where(edge_lo, 0.0, pltpu.roll(left, 1, 0))
        right_carry = jnp.where(edge_hi, 0.0, pltpu.roll(right, SUB - 1, 0))
        return jnp.where(lane_lo, left_carry, left) + jnp.where(lane_hi, right_carry, right)

    def recursion(d, order):
        count = -(-(rows + MARGIN - order) // UNROLL) * UNROLL
        first = jnp.where(ti == 0, MARGIN, MARGIN + rows - count)

        def this_at(f, r):
            return base[d, f, r] if order == 1 else terms[order - 2, f, r]

        def prev_at(f, r):
            return base[d, f, r] if order == 2 else terms[order - 3, f, r]

        def body(i, carry):
            r0 = first + i * UNROLL
            for f in range(4):
                p = [this_at(f, r0 + k - 1) for k in range(UNROLL + 2)]
                for k in range(UNROLL):
                    twice = p[k + 1] + p[k + 1]
                    along_x = (p[k] + p[k + 2]) + twice
                    both = neighbours(along_x) + (along_x + along_x)
                    if order == 1:
                        value = 0.125 * both - p[k + 1]
                    else:
                        value = 0.25 * both - (twice + prev_at(f, r0 + k))
                    terms[order - 1, f, r0 + k] = value
            return carry

        lax.fori_loop(0, count // UNROLL, body, 0)

    omega = omega_ref[0]

    def slow_row(d, r):
        if cols == LANE:
            tile = [gathered[f, d, pl.ds(r, 1), :] for f in range(n)]
            return jnp.concatenate(tile, axis=0)
        per = LANE // cols
        return jnp.concatenate([
            jnp.concatenate([gathered[s * per + q, d, pl.ds(r, 1), :] for q in range(per)], axis=1)
            for s in range(SUB)], axis=0)

    def accumulate(d, lo, hi):
        def body(i, carry):
            r = jnp.where(ti == 0, rows - 1 - i, i)
            h = folded_coefficients(slow_row(d, r) * omega)
            sr = si = rr = ri = None
            for t in range(TERMS):
                v = [base[d, f, MARGIN + r] if t == 0 else terms[t - 1, f, MARGIN + r] for f in range(4)]
                hv = [h[t] * x for x in v]
                if t == 0:
                    sr, si, rr, ri = hv
                elif t % 2 == 0:
                    sr, si, rr, ri = sr + hv[0], si + hv[1], rr + hv[2], ri + hv[3]
                else:
                    sr, si, rr, ri = sr - hv[1], si + hv[0], rr + hv[3], ri - hv[2]
            if d + 1 < steps:
                for f, x in enumerate((sr, si, rr, ri)):
                    base[d + 1, f, MARGIN + r] = x
            part[d, 0, r] = sr * rr + si * ri
            part[d, 1, r] = sr * sr + si * si
            return carry

        lax.fori_loop(lo, hi, body, 0)

    def s1_copy(d):
        return pltpu.make_async_remote_copy(
            src_ref=part.at[d, :, pl.ds(other_y * half, half)], dst_ref=recv1.at[d],
            send_sem=s1_send.at[d], recv_sem=s1_recv.at[d],
            device_id=freq_at(other_y, zi), device_id_type=MESH)

    def s2_copy(d, z, slot):
        return pltpu.make_async_remote_copy(
            src_ref=acc1.at[d, :, pl.ds(z * chunk, chunk)], dst_ref=recv2.at[d, slot],
            send_sem=s2_send.at[d, z], recv_sem=s2_recv.at[d, slot],
            device_id=freq_at(yi, z), device_id_type=MESH)

    def piece(d, y, z):
        return result.at[d, :, pl.ds(y * half + z * chunk, chunk)]

    def gz_copy(d, owner, target):
        return pltpu.make_async_remote_copy(
            src_ref=piece(d, yi, owner), dst_ref=piece(d, yi, owner),
            send_sem=gz_send.at[d, target], recv_sem=gz_recv.at[d, owner],
            device_id=freq_at(yi, target), device_id_type=MESH)

    def gy_copy(d, y, z):
        return pltpu.make_async_remote_copy(
            src_ref=piece(d, y, z), dst_ref=piece(d, y, z),
            send_sem=gy_send.at[d, z], recv_sem=gy_recv.at[d, z],
            device_id=freq_at(other_y, zi), device_id_type=MESH)

    peers = [lax.rem(zi + j, g2) for j in range(1, g2)]

    def stage_b(d):
        s1_copy(d).wait_recv()

        def body(r, carry):
            for a in range(2):
                acc1[d, a, r] = part[d, a, yi * half + r] + recv1[d, a, r]
            return carry

        lax.fori_loop(0, half, body, 0)
        for z in peers:
            s2_copy(d, z, zi).start()

    scale = (1.0 / math.sqrt(freq_total), 1.0 / freq_total)

    def stage_c(d):
        for z in peers:
            s2_copy(d, zi, z).wait_recv()
        for a in range(2):
            for r in range(chunk):
                total = acc1[d, a, zi * chunk + r]
                for z in peers:
                    total = total + recv2[d, z, a, r]
                result[d, a, yi * half + zi * chunk + r] = total * scale[a]
        for z in peers:
            gz_copy(d, zi, z).start()
        gy_copy(d, yi, zi).start()

    def stage_d(d):
        for z in peers:
            gz_copy(d, z, zi).wait_recv()
            gy_copy(d, yi, z).start()

    def out_copy(d):
        return pltpu.make_async_copy(result.at[d], out_ref.at[d], out_sem.at[d])

    def stage_e(d):
        for z in range(g2):
            gy_copy(d, other_y, z).wait_recv()
        out_copy(d).start()

    for d in range(steps):
        for copy in halo_copies(d):
            copy.wait_recv()
        for order in range(1, TERMS):
            recursion(d, order)
            if order == 3 and d >= 1:
                stage_b(d - 1)
            if order == 6 and d >= 1:
                stage_c(d - 1)
        if d >= 1:
            stage_d(d - 1)
        if d == 0:
            loads[2].wait()
        for j in range(1, n):
            slow_copy(d, lax.rem(fi + j, n), j, fi).wait_recv()
        accumulate(d, 0, MARGIN)
        if d + 1 < steps:
            for copy in halo_copies(d + 1):
                copy.start()
        accumulate(d, MARGIN, rows)
        s1_copy(d).start()
        if d >= 1:
            stage_e(d - 1)
    last = steps - 1
    stage_b(last)
    stage_c(last)
    stage_d(last)
    stage_e(last)

    for d in range(steps):
        for copy in halo_copies(d):
            copy.wait_send()
        for j in range(1, n):
            slow_copy(d, fi, j, lax.rem(fi + j, n)).wait_send()
        s1_copy(d).wait_send()
        for z in peers:
            s2_copy(d, z, zi).wait_send()
            gz_copy(d, zi, z).wait_send()
        for z in range(g2):
            gy_copy(d, yi, z).wait_send()
        out_copy(d).wait()


def per_device(n, source_field, receiver_field, slowness, omegas):
    rows, width = source_field.shape[2:]
    steps, _, cols = slowness.shape
    g1 = 2
    g2 = n // g1
    half, chunk = rows // g1, rows // n
    height = rows + 2 * MARGIN
    f32, dma = jnp.float32, pltpu.SemaphoreType.DMA
    src = source_field.reshape(2, rows, SUB, LANE)
    rec = receiver_field.reshape(2, rows, SUB, LANE)
    cfg = (n, g1, g2, rows, steps, omegas.shape[0] * n, cols)
    any_spec = pl.BlockSpec(memory_space=pl.ANY)
    out = pl.pallas_call(
        functools.partial(kernel, cfg),
        out_shape=jax.ShapeDtypeStruct((steps, 2, rows, SUB, LANE), f32),
        in_specs=[any_spec, any_spec, any_spec, pl.BlockSpec(memory_space=pltpu.SMEM)],
        out_specs=any_spec,
        scratch_shapes=[
            pltpu.VMEM((steps, 4, height, SUB, LANE), f32),
            pltpu.VMEM((TERMS - 1, 4, height, SUB, LANE), f32),
            pltpu.VMEM((n, steps, rows, cols), f32),
            pltpu.VMEM((steps, 2, rows, SUB, LANE), f32),
            pltpu.VMEM((steps, 2, half, SUB, LANE), f32),
            pltpu.VMEM((steps, 2, half, SUB, LANE), f32),
            pltpu.VMEM((steps, g2, 2, chunk, SUB, LANE), f32),
            pltpu.VMEM((steps, 2, rows, SUB, LANE), f32),
            dma((2,)), dma(()), dma((steps,)),
            dma((steps, n)), dma((steps, n)),
            dma((steps, 2)), dma((steps, 2)),
            dma((steps,)), dma((steps,)),
            dma((steps, g2)), dma((steps, g2)),
            dma((steps, g2)), dma((steps, g2)),
            dma((steps, g2)), dma((steps, g2)),
        ],
        compiler_params=pltpu.CompilerParams(
            collective_id=0, has_side_effects=True, vmem_limit_bytes=48 * 1024 * 1024),
    )(src, rec, slowness, omegas)
    return (out[:, 0].reshape(steps, rows, width), out[:, 1].reshape(steps, rows, width))


def solution(mesh):
    n = mesh.shape["freq"]
    assert mesh.shape["tile"] == 2 and n % 2 == 0
    in_specs = (
        P("shot", "freq", "tile", None),
        P("shot", "freq", "tile", None),
        P(None, "tile", "freq"),
        P("freq"),
    )
    out_specs = (P("shot", "tile", None), P("shot", "tile", None))
    return jax.shard_map(
        functools.partial(per_device, n), mesh=mesh, in_specs=in_specs, out_specs=out_specs,
        check_vma=False,
    )
```

```python
import functools
import math

import jax
import jax.numpy as jnp
import numpy as np
from jax import lax
from jax.experimental import pallas as pl
from jax.experimental.pallas import tpu as pltpu
from jax.sharding import PartitionSpec as P

TERMS = 10
NODES = 16
MARGIN = TERMS - 1
HALF = NODES // 2
SUB, LANE = 8, 128
MESH = pl.DeviceIdType.MESH
UNROLL = 8
LAGS = (4, 9, 14, 17)

SIN_POLY = (3.14159258, -5.16770688, 2.55003137, -0.59804516, 0.07722009)
COS_POLY = (0.99999995, -4.93479286, 4.0584119, -1.33188005, 0.21969657)


def horner(coefs, z):
    out = coefs[-1] * z + coefs[-2]
    for c in reversed(coefs[:-2]):
        out = out * z + c
    return out


def folded_coefficients(u):
    theta = [math.pi * (m + 0.5) / NODES for m in range(HALF)]
    cosines, sines = [], []
    for m in range(HALF):
        y = u * (math.cos(theta[m]) / (2 * math.pi))
        g = y - jnp.round(y)
        z = g * g
        s = horner(SIN_POLY, z) * g
        c = horner(COS_POLY, z)
        twice = s + s
        cosines.append(1.0 - twice * s)
        sines.append(twice * c)
    weight = [2.0 * (1.0 if n == 0 else 2.0) / NODES for n in range(TERMS)]
    out = [None] * TERMS
    sums = [cosines[m] + cosines[HALF - 1 - m] for m in range(HALF // 2)]
    diffs = [cosines[m] - cosines[HALF - 1 - m] for m in range(HALF // 2)]
    for n in range(0, TERMS, 2):
        terms = sums if (n // 2) % 2 == 0 else diffs
        total = None
        for m in range(HALF // 2):
            term = terms[m] * (weight[n] * math.cos(n * theta[m]))
            total = term if total is None else total + term
        out[n] = total
    for n in range(1, TERMS, 2):
        total = None
        for m in range(HALF):
            term = sines[m] * (weight[n] * math.cos(n * theta[m]))
            total = term if total is None else total + term
        out[n] = total
    return out


def kernel(cfg, src_ref, rec_ref, slow_ref, omega_ref, out_ref, base, terms, gathered, part,
           recv1, acc1, recv2, result, load_sem, own_sem, out_sem, slow_send, slow_recv,
           halo_send, halo_recv, s1_send, s1_recv, s2_send, s2_recv,
           gz_send, gz_recv, gy_send, gy_recv):
    n, g1, g2, rows, steps, freq_total, cols, group = cfg
    chunk = group // g2
    groups = rows // group
    units = steps * groups
    fi = lax.axis_index("freq")
    ti = lax.axis_index("tile")
    yi, zi = lax.rem(fi, g1), lax.div(fi, g1)
    other_y = g1 - 1 - yi

    def freq_at(y, z):
        return {"freq": z * g1 + y}

    loads = [
        pltpu.make_async_copy(src_ref, base.at[0, 0:2, pl.ds(MARGIN, rows)], load_sem.at[0]),
        pltpu.make_async_copy(rec_ref, base.at[0, 2:4, pl.ds(MARGIN, rows)], load_sem.at[1]),
        pltpu.make_async_copy(slow_ref, gathered.at[fi], own_sem),
    ]
    for copy in loads:
        copy.start()

    barrier = pltpu.get_barrier_semaphore()
    for j in range(1, n):
        pl.semaphore_signal(barrier, inc=1, device_id={"freq": lax.rem(fi + j, n)}, device_id_type=MESH)
    pl.semaphore_signal(barrier, inc=1, device_id={"tile": 1 - ti}, device_id_type=MESH)

    zero_row = jnp.where(ti == 0, MARGIN - 1, MARGIN + rows)
    zero = jnp.zeros((SUB, LANE), jnp.float32)
    for f in range(4):
        for d in range(steps):
            base[d, f, zero_row] = zero
        for t in range(TERMS - 1):
            terms[t, f, zero_row] = zero

    pl.semaphore_wait(barrier, n)

    in_start = jnp.where(ti == 0, rows - MARGIN, 0)
    halo_src = in_start + MARGIN
    halo_dst = jnp.where(ti == 0, 0, MARGIN + rows)

    def halo_copies(d):
        dst = pl.ds(halo_dst, MARGIN)
        if d == 0:
            pairs = [
                (src_ref.at[:, pl.ds(in_start, MARGIN)], base.at[0, 0:2, dst]),
                (rec_ref.at[:, pl.ds(in_start, MARGIN)], base.at[0, 2:4, dst]),
            ]
        else:
            pairs = [
                (base.at[d, 0:2, pl.ds(halo_src, MARGIN)], base.at[d, 0:2, dst]),
                (base.at[d, 2:4, pl.ds(halo_src, MARGIN)], base.at[d, 2:4, dst]),
            ]
        return [
            pltpu.make_async_remote_copy(
                src_ref=a, dst_ref=b, send_sem=halo_send.at[d, i], recv_sem=halo_recv.at[d, i],
                device_id={"tile": 1 - ti}, device_id_type=MESH)
            for i, (a, b) in enumerate(pairs)
        ]

    def slow_copy(d, slot, j, target):
        return pltpu.make_async_remote_copy(
            src_ref=slow_ref.at[d], dst_ref=gathered.at[slot, d],
            send_sem=slow_send.at[d, j], recv_sem=slow_recv.at[d, slot],
            device_id={"freq": target}, device_id_type=MESH)

    for copy in halo_copies(0):
        copy.start()
    for d in range(steps):
        for j in range(1, n):
            slow_copy(d, fi, j, lax.rem(fi + j, n)).start()

    for copy in loads[:2]:
        copy.wait()

    lane = lax.broadcasted_iota(jnp.int32, (SUB, LANE), 1)
    sub = lax.broadcasted_iota(jnp.int32, (SUB, LANE), 0)
    lane_lo, lane_hi = lane == 0, lane == LANE - 1
    edge_lo, edge_hi = sub == 0, sub == SUB - 1

    def neighbours(v):
        left = pltpu.roll(v, 1, 1)
        right = pltpu.roll(v, LANE - 1, 1)
        left_carry = jnp.where(edge_lo, 0.0, pltpu.roll(left, 1, 0))
        right_carry = jnp.where(edge_hi, 0.0, pltpu.roll(right, SUB - 1, 0))
        return jnp.where(lane_lo, left_carry, left) + jnp.where(lane_hi, right_carry, right)

    def recursion(d, k, order):
        offset = 0 if k == 0 else k * group + MARGIN - order
        count = group + (MARGIN - order if k == 0 else 0)
        count = -(-count // UNROLL) * UNROLL
        first = jnp.where(ti == 0, MARGIN + offset, MARGIN + rows - offset - count)

        def this_at(f, r):
            return base[d, f, r] if order == 1 else terms[order - 2, f, r]

        def prev_at(f, r):
            return base[d, f, r] if order == 2 else terms[order - 3, f, r]

        def body(i, carry):
            r0 = first + i * UNROLL
            for f in range(4):
                p = [this_at(f, r0 + k - 1) for k in range(UNROLL + 2)]
                for k in range(UNROLL):
                    twice = p[k + 1] + p[k + 1]
                    along_x = (p[k] + p[k + 2]) + twice
                    both = neighbours(along_x) + (along_x + along_x)
                    if order == 1:
                        value = 0.125 * both - p[k + 1]
                    else:
                        value = 0.25 * both - (twice + prev_at(f, r0 + k))
                    terms[order - 1, f, r0 + k] = value
            return carry

        lax.fori_loop(0, count // UNROLL, body, 0)

    omega = omega_ref[0]

    def slow_row(d, r):
        if cols == LANE:
            tile = [gathered[f, d, pl.ds(r, 1), :] for f in range(n)]
            return jnp.concatenate(tile, axis=0)
        per = LANE // cols
        return jnp.concatenate([
            jnp.concatenate([gathered[s * per + q, d, pl.ds(r, 1), :] for q in range(per)], axis=1)
            for s in range(SUB)], axis=0)

    def accumulate(d, k):
        unit = d * groups + k

        def body(i, carry):
            r = jnp.where(ti == 0, k * group + i, rows - (k + 1) * group + i)
            h = folded_coefficients(slow_row(d, r) * omega)
            sr = si = rr = ri = None
            for t in range(TERMS):
                v = [base[d, f, MARGIN + r] if t == 0 else terms[t - 1, f, MARGIN + r] for f in range(4)]
                hv = [h[t] * x for x in v]
                if t == 0:
                    sr, si, rr, ri = hv
                elif t % 2 == 0:
                    sr, si, rr, ri = sr + hv[0], si + hv[1], rr + hv[2], ri + hv[3]
                else:
                    sr, si, rr, ri = sr - hv[1], si + hv[0], rr + hv[3], ri - hv[2]
            if d + 1 < steps:
                for f, x in enumerate((sr, si, rr, ri)):
                    base[d + 1, f, MARGIN + r] = x
            part[unit, 0, i] = sr * rr + si * ri
            part[unit, 1, i] = sr * sr + si * si
            return carry

        lax.fori_loop(0, group, body, 0)

    def s1_copy(u):
        return pltpu.make_async_remote_copy(
            src_ref=part.at[u, other_y], dst_ref=recv1.at[u],
            send_sem=s1_send.at[u], recv_sem=s1_recv.at[u],
            device_id=freq_at(other_y, zi), device_id_type=MESH)

    def s2_copy(u, z, slot):
        return pltpu.make_async_remote_copy(
            src_ref=acc1.at[u, pl.ds(z * chunk, chunk)], dst_ref=recv2.at[u, slot],
            send_sem=s2_send.at[u, z], recv_sem=s2_recv.at[u, slot],
            device_id=freq_at(yi, z), device_id_type=MESH)

    def row_start(u):
        d, k = u // groups, u % groups
        return d, jnp.where(ti == 0, k * group, rows - (k + 1) * group)

    def piece(u, y, z):
        d, start = row_start(u)
        return result.at[y, d, pl.ds(start + z * chunk, chunk)]

    def gz_copy(u, owner, target):
        return pltpu.make_async_remote_copy(
            src_ref=piece(u, yi, owner), dst_ref=piece(u, yi, owner),
            send_sem=gz_send.at[u, target], recv_sem=gz_recv.at[u, owner],
            device_id=freq_at(yi, target), device_id_type=MESH)

    def gy_copy(u, y, z):
        return pltpu.make_async_remote_copy(
            src_ref=piece(u, y, z), dst_ref=piece(u, y, z),
            send_sem=gy_send.at[u, z], recv_sem=gy_recv.at[u, z],
            device_id=freq_at(other_y, zi), device_id_type=MESH)

    peers = [lax.rem(zi + j, g2) for j in range(1, g2)]

    def stage_b(u):
        s1_copy(u).wait_recv()

        def body(r, carry):
            acc1[u, r] = part[u, yi, r] + recv1[u, r]
            return carry

        lax.fori_loop(0, group, body, 0, unroll=4)
        for z in peers:
            s2_copy(u, z, zi).start()

    scale = jnp.where(yi == 0, 1.0 / math.sqrt(freq_total), 1.0 / freq_total)

    def stage_c(u):
        for z in peers:
            s2_copy(u, zi, z).wait_recv()
        d, start = row_start(u)
        for r in range(chunk):
            total = acc1[u, zi * chunk + r]
            for z in peers:
                total = total + recv2[u, z, r]
            result[yi, d, start + zi * chunk + r] = total * scale
        for z in peers:
            gz_copy(u, zi, z).start()
        gy_copy(u, yi, zi).start()

    def stage_d(u):
        for z in peers:
            gz_copy(u, z, zi).wait_recv()
            gy_copy(u, yi, z).start()

    def out_copy(u):
        d, start = row_start(u)
        rows_of = pl.ds(start, group)
        return pltpu.make_async_copy(result.at[:, d, rows_of], out_ref.at[:, d, rows_of], out_sem.at[u])

    def stage_e(u):
        for z in range(g2):
            gy_copy(u, other_y, z).wait_recv()
        out_copy(u).start()

    queue = sorted(
        (3 * u + 3 + lag, u, stage)
        for u in range(units)
        for lag, stage in ((LAGS[0], 0), (LAGS[1], 1), (LAGS[2], 2), (LAGS[3], 3)))
    stages = (stage_b, stage_c, stage_d, stage_e)

    def poll(tick):
        while queue and (tick is None or queue[0][0] <= tick):
            _, u, stage = queue.pop(0)
            stages[stage](u)

    for d in range(steps):
        waited = False
        for k in range(groups):
            u = d * groups + k
            if not waited and (k + 1) * group + MARGIN > rows:
                waited = True
                for copy in halo_copies(d):
                    copy.wait_recv()
            for order in range(1, TERMS):
                recursion(d, k, order)
                if order == 4:
                    poll(3 * u + 1)
            poll(3 * u + 2)
            if k == 0:
                if d == 0:
                    loads[2].wait()
                for j in range(1, n):
                    slow_copy(d, lax.rem(fi + j, n), j, fi).wait_recv()
            accumulate(d, k)
            s1_copy(u).start()
            if k == groups - 1 and d + 1 < steps:
                for copy in halo_copies(d + 1):
                    copy.start()
            poll(3 * u + 3)
    poll(None)

    for d in range(steps):
        for copy in halo_copies(d):
            copy.wait_send()
        for j in range(1, n):
            slow_copy(d, fi, j, lax.rem(fi + j, n)).wait_send()
    for u in range(units):
        s1_copy(u).wait_send()
        for z in peers:
            s2_copy(u, z, zi).wait_send()
            gz_copy(u, zi, z).wait_send()
        for z in range(g2):
            gy_copy(u, yi, z).wait_send()
        out_copy(u).wait()


def per_device(n, source_field, receiver_field, slowness, omegas):
    rows, width = source_field.shape[2:]
    steps, _, cols = slowness.shape
    g1 = 2
    g2 = n // g1
    group = max(rows // 2, n // 2)
    units, chunk = steps * (rows // group), group // g2
    height = rows + 2 * MARGIN
    f32, dma = jnp.float32, pltpu.SemaphoreType.DMA
    src = source_field.reshape(2, rows, SUB, LANE)
    rec = receiver_field.reshape(2, rows, SUB, LANE)
    cfg = (n, g1, g2, rows, steps, omegas.shape[0] * n, cols, group)
    any_spec = pl.BlockSpec(memory_space=pl.ANY)
    out = pl.pallas_call(
        functools.partial(kernel, cfg),
        out_shape=jax.ShapeDtypeStruct((2, steps, rows, SUB, LANE), f32),
        in_specs=[any_spec, any_spec, any_spec, pl.BlockSpec(memory_space=pltpu.SMEM)],
        out_specs=any_spec,
        scratch_shapes=[
            pltpu.VMEM((steps, 4, height, SUB, LANE), f32),
            pltpu.VMEM((TERMS - 1, 4, height, SUB, LANE), f32),
            pltpu.VMEM((n, steps, rows, cols), f32),
            pltpu.VMEM((units, 2, group, SUB, LANE), f32),
            pltpu.VMEM((units, group, SUB, LANE), f32),
            pltpu.VMEM((units, group, SUB, LANE), f32),
            pltpu.VMEM((units, g2, chunk, SUB, LANE), f32),
            pltpu.VMEM((2, steps, rows, SUB, LANE), f32),
            dma((2,)), dma(()), dma((units,)),
            dma((steps, n)), dma((steps, n)),
            dma((steps, 2)), dma((steps, 2)),
            dma((units,)), dma((units,)),
            dma((units, g2)), dma((units, g2)),
            dma((units, g2)), dma((units, g2)),
            dma((units, g2)), dma((units, g2)),
        ],
        compiler_params=pltpu.CompilerParams(
            collective_id=0, has_side_effects=True, vmem_limit_bytes=48 * 1024 * 1024),
    )(src, rec, slowness, omegas)
    return (out[0].reshape(steps, rows, width), out[1].reshape(steps, rows, width))


def solution(mesh):
    n = mesh.shape["freq"]
    assert mesh.shape["tile"] == 2 and n % 2 == 0
    in_specs = (
        P("shot", "freq", "tile", None),
        P("shot", "freq", "tile", None),
        P(None, "tile", "freq"),
        P("freq"),
    )
    out_specs = (P("shot", "tile", None), P("shot", "tile", None))
    return jax.shard_map(
        functools.partial(per_device, n), mesh=mesh, in_specs=in_specs, out_specs=out_specs,
        check_vma=False,
    )
```
